32 devices in a mesh: blk: 8 (over z, x), view: 4 (over y, core).
Axes of the slice: x: 2, y: 2, z: 4, core: 2. Of those that a mesh axis runs over, the one named last changes fastest.
Arguments:
- estimate: float32 [256, 256, 256], P('blk'), may hold values from 0.5 to 2
- tiles: float32 [4, 512, 32, 256], P('view', 'blk'), may hold values from 0.1 to 10
- tile_dest: int32 [4, 512, 1], P('view'), may hold values from 0 to 7; in each aligned block of 64 rows (0 to 63, 64 to 127, ..., all dimensions but the last counted through in order) at most 16 rows name the same one
- tile_plane: int32 [4, 512], P('view'), may hold values from 0 to 31
- tile_row: int32 [4, 512], P('view'), may hold values from 0 to 224
- psf: float32 [4, 3, 31], replicated, may hold values from 0.05 to 1
- view_shift: int32 [4, 2], replicated, may hold values from -8 to 8
Outputs:
- joined: float32 [256, 256, 256], P('blk')
The draws below stay inside these ranges and needn't reach their ends.
Inputs may be any that keep to these rules, and one draw needn't show every extreme that they name: `tile_dest`: among the tiles of one view in an aligned block of 64 tiles (the tiles of one index of blk), at most 16 land in any one block, and in every draw some block receives exactly 16 of them.
All inputs are finite; a program needn't handle non-finite values.
Results may differ from the reference program's by a relative error of at most 0.0003.
Values sent between devices are 32-bit elements; how exact they have to be, the bound alone decides.
A program may use at most 128 MiB of HBM per device.

```python
import math
import jax
import jax.numpy as jnp
import numpy as np
from jax import lax

CZ = 32
NY = 256
NX = 256
TR = 32
TILE_DEV = 64
TAPS = 31
SHIFT = 8
ITERS = 1
RADIUS = 15
VIEWS = 4
NZ = 256
TILES = 512
CAP = 16
N_BLK = 8


def place_ends(result, key, low, largest):
    dims = result.shape
    spot = [jax.random.randint(jax.random.fold_in(key, axis), (), 0, dims[axis]) for axis in range(len(dims))]
    result = result.at[tuple(spot)].set(low)
    longest = dims.index(max(dims))
    spot[longest] = (spot[longest] + 1) % dims[longest]
    return result.at[tuple(spot)].set(largest)


def block_scale(own_key, dims, shards, smallest, largest):
    loudness, own = 1.0, jax.random.fold_in(own_key, 6)
    for position, parts in shards:
        draws = jnp.exp(jax.random.uniform(jax.random.fold_in(own, position), (parts,), jnp.float32, smallest / len(shards), largest / len(shards)))
        loudness = loudness * jnp.repeat(draws, dims[position] // parts).reshape([-1 if axis == position else 1 for axis in range(len(dims))])
    return loudness


def shared_out(key, own, number, rows, amount, top, bound, skew):
    ranking = jax.random.permutation(key, amount)
    crowded, common = shares(amount, rows * top, bound, skew, True), shares(amount, rows * top, bound, skew, False)
    places = jnp.arange(amount)

    def named(sizes, rotation):
        used = int((sizes > 0).sum())
        fixed = max(1, used // 4)
        passed = fixed + (places - fixed + rotation * (used - fixed)) % max(1, amount - fixed)
        return jnp.zeros((amount,), jnp.int32).at[ranking[jnp.where(places < fixed, places, passed)]].set(jnp.asarray(sizes, jnp.int32))

    sizes = jnp.where(number % 4 == 0, named(crowded, number // 4), named(common, number - number // 4 - 1))
    mixed = jax.random.permutation(jax.random.fold_in(own, 3), amount)
    source_of, sink = mixed[0:amount // 2 * 2:2], mixed[1:amount // 2 * 2:2]
    slack = jnp.minimum(sizes[source_of] - 1, bound - sizes[sink]) // 2
    slack = jnp.where((source_of == ranking[0]) | (sink == ranking[0]) | (sizes[sink] == 0), 0, jnp.maximum(slack, 0))
    passed = jax.random.randint(jax.random.fold_in(own, 4), (amount // 2,), 0, 1 << 20) % (slack + 1)
    sizes = sizes.at[source_of].add(-passed).at[sink].add(passed)
    items = jnp.searchsorted(jnp.cumsum(sizes), jnp.arange(rows * top), side="right").astype(jnp.int32)
    grid = items.reshape(top, rows).T
    grid = grid[jax.random.permutation(jax.random.fold_in(own, 1), rows)]
    rotation = jax.random.randint(jax.random.fold_in(own, 2), (rows, 1), 0, top)
    return jnp.take_along_axis(grid, (jnp.arange(top)[None, :] + rotation) % top, axis=1)


def shares(number_of, total, limit, lean, full):
    portions = [(1 << 20) // math.isqrt(rank ** lean) + 1 for rank in range(1, number_of + 1)]
    largest = limit if full else min(limit, max(-(-total // number_of), total * portions[0] // sum(portions)))
    least = 1 if total - largest >= number_of - 1 else 0
    counts, surplus = [largest] + [least] * (number_of - 1), total - largest - least * (number_of - 1)
    while surplus > 0:
        movable = [i for i in range(1, number_of) if counts[i] < largest] or [i for i in range(1, number_of) if counts[i] < limit]
        mass, left = sum([portions[i] for i in movable]), surplus
        for i in movable:
            extra = min(limit - counts[i], max(1, left * portions[i] // mass), surplus)
            counts[i] = counts[i] + extra
            surplus = surplus - extra
    return np.array(counts)


def setup_inputs(seed: int = 0) -> dict:
    streams_of = jax.random.split(jax.random.key(seed), 8)
    estimate = jnp.clip(jnp.exp(math.log(2.0) - 1.3862944 * jax.random.uniform(streams_of[0], (NZ, NY, NX), jnp.float32) ** block_scale(streams_of[0], (NZ, NY, NX), ((0, 8),), -0.2, 0.2)), 0.5, 2.0)
    tiles = jnp.clip(jnp.exp(math.log(10.0) - 4.6051702 * jax.random.uniform(streams_of[1], (VIEWS, TILES, TR, NX), jnp.float32) ** block_scale(streams_of[1], (VIEWS, TILES, TR, NX), ((0, 4), (1, 8)), -0.2, 0.2)), 0.1, 10.0)
    tile_dest_keys = jax.random.split(jax.random.fold_in(streams_of[2], 1), VIEWS * TILES // TILE_DEV)
    tile_dest_turns = jax.random.permutation(jax.random.fold_in(streams_of[2], 3), VIEWS * TILES // TILE_DEV)
    tile_dest = jax.vmap(lambda own, number: shared_out(jax.random.fold_in(streams_of[2], 2), own, number, TILE_DEV, N_BLK, 1, CAP, 2))(tile_dest_keys, tile_dest_turns).reshape((VIEWS, TILES, 1))
    tile_plane = place_ends(jax.random.randint(streams_of[3], (VIEWS, TILES), 0, CZ), jax.random.fold_in(streams_of[3], 1), 0, CZ - 1).astype(jnp.int32)
    tile_row = place_ends(jax.random.randint(streams_of[4], (VIEWS, TILES), 0, NY - TR + 1), jax.random.fold_in(streams_of[4], 1), 0, NY - TR).astype(jnp.int32)
    psf = jnp.clip(jnp.exp(jax.random.uniform(streams_of[5], (VIEWS, 3, TAPS), jnp.float32, math.log(0.05), math.log(1.0))), 0.05, 1.0)
    view_shift = place_ends(jax.random.randint(streams_of[6], (VIEWS, 2), 0 - SHIFT, SHIFT + 1), jax.random.fold_in(streams_of[6], 1), 0 - SHIFT, SHIFT).astype(jnp.int32)
    return dict(estimate=estimate, tiles=tiles, tile_dest=tile_dest, tile_plane=tile_plane, tile_row=tile_row, psf=psf, view_shift=view_shift)


HIGH = lax.Precision.HIGHEST
BACKGROUND = 0.05


def normalize(psf):
    return psf / jnp.sum(psf, axis=-1, keepdims=True)


def lateral_matrix(kernel, shift, count):
    outputs = jnp.arange(count, dtype=jnp.int32)[:, None]
    inputs = jnp.arange(count, dtype=jnp.int32)[None, :]
    offset = inputs - outputs + (TAPS - 1) // 2 - shift
    taps = jnp.arange(TAPS, dtype=jnp.int32)
    hits = (offset[:, :, None] == taps[None, None, :]).astype(jnp.float32)
    return jnp.einsum("oit,t->oi", hits, kernel.astype(jnp.float32), precision=HIGH)


def band_matrix(kernel, rows):
    outputs = jnp.arange(rows, dtype=jnp.int32)[:, None]
    inputs = jnp.arange(rows + TAPS - 1, dtype=jnp.int32)[None, :]
    offset = inputs - outputs
    taps = jnp.arange(TAPS, dtype=jnp.int32)
    hits = (offset[:, :, None] == taps[None, None, :]).astype(jnp.float32)
    return jnp.einsum("oit,t->oi", hits, kernel.astype(jnp.float32), precision=HIGH)


def coverage(kernel, shift, count, first, total):
    places = first + jnp.arange(count, dtype=jnp.int32)
    taps = jnp.arange(TAPS, dtype=jnp.int32)
    source = places[:, None] - taps[None, :] + (TAPS - 1) // 2 - shift
    inside = ((source >= 0) & (source < total)).astype(jnp.float32)
    return jnp.sum(inside * kernel[None, :], axis=1)


def along_z(volume, band):
    padded = jnp.pad(volume, ((RADIUS, RADIUS), (0, 0), (0, 0)))

    def one_block(index):
        piece = lax.dynamic_slice_in_dim(padded, index * CZ, CZ + 2 * RADIUS, 0)
        return jnp.einsum("oi,iyx->oyx", band, piece, precision=HIGH)

    blocks = lax.map(one_block, jnp.arange(N_BLK, dtype=jnp.int32))
    return blocks.reshape(NZ, NY, NX)


def lateral(volume, matrix_y, matrix_x):
    moved = jnp.einsum("yi,zix->zyx", matrix_y, volume, precision=HIGH)
    return jnp.einsum("zyi,xi->zyx", moved, matrix_x, precision=HIGH)


def lateral_back(volume, matrix_y, matrix_x):
    moved = jnp.einsum("iy,zix->zyx", matrix_y, volume, precision=HIGH)
    return jnp.einsum("zyi,ix->zyx", moved, matrix_x, precision=HIGH)


def assemble(tiles_view, target, plane, first_row):
    start = (target * CZ + plane) * NY + first_row
    flat = (start[:, None] + jnp.arange(TR, dtype=jnp.int32)[None, :]).reshape(-1)
    values = tiles_view.reshape(TILES * TR, NX)
    total = jnp.zeros((NZ * NY, NX), jnp.float32).at[flat].add(values)
    count = jnp.zeros((NZ * NY,), jnp.float32).at[flat].add(1.0)
    return (total / jnp.maximum(count, 1.0)[:, None]).reshape(NZ, NY, NX)


def reference(estimate, tiles, tile_dest, tile_plane, tile_row, psf, view_shift):
    kernels = normalize(psf)
    data = []
    forward_bands = []
    back_bands = []
    matrices = []
    sensitivity = jnp.zeros((NZ, NY, NX), jnp.float32)
    for other in range(VIEWS):
        data.append(assemble(tiles[other], tile_dest[other, :, 0], tile_plane[other], tile_row[other]))
        forward_bands.append(band_matrix(kernels[other, 0], CZ))
        back_bands.append(band_matrix(kernels[other, 0][::-1], CZ))
        matrices.append((lateral_matrix(kernels[other, 1], view_shift[other, 0], NY),
                         lateral_matrix(kernels[other, 2], view_shift[other, 1], NX)))
        cover_z = coverage(kernels[other, 0], 0, NZ, 0, NZ)
        cover_y = coverage(kernels[other, 1], view_shift[other, 0], NY, 0, NY)
        cover_x = coverage(kernels[other, 2], view_shift[other, 1], NX, 0, NX)
        sensitivity = sensitivity + cover_z[:, None, None] * cover_y[None, :, None] * cover_x[None, None, :]
    joined = estimate
    for step in range(ITERS):
        summed = jnp.zeros((NZ, NY, NX), jnp.float32)
        for other in range(VIEWS):
            image = lateral(along_z(joined, forward_bands[other]), matrices[other][0], matrices[other][1])
            ratio = data[other] / (image + BACKGROUND)
            summed = summed + lateral_back(along_z(ratio, back_bands[other]), matrices[other][0], matrices[other][1])
        joined = joined * summed / sensitivity
    return joined
```

```python
import jax
import jax.numpy as jnp
from jax import lax
from jax.experimental import pallas as pl
from jax.experimental.pallas import tpu as pltpu
from jax.sharding import PartitionSpec as P

TAPS = 31


HIGH = lax.Precision.HIGHEST
NEAR = lax.Precision.HIGH
BACKGROUND = 0.05
CHUNKS = 4


def normalize(psf):
    return psf / jnp.sum(psf, axis=-1, keepdims=True)


def lateral_matrix(kernel, shift, count):
    outputs = jnp.arange(count, dtype=jnp.int32)[:, None]
    inputs = jnp.arange(count, dtype=jnp.int32)[None, :]
    offset = inputs - outputs + (TAPS - 1) // 2 - shift
    taps = jnp.arange(TAPS, dtype=jnp.int32)
    hits = (offset[:, :, None] == taps[None, None, :]).astype(jnp.float32)
    return jnp.einsum("oit,t->oi", hits, kernel, precision=HIGH)


def band_matrix(kernel, rows):
    outputs = jnp.arange(rows, dtype=jnp.int32)[:, None]
    inputs = jnp.arange(rows + TAPS - 1, dtype=jnp.int32)[None, :]
    offset = inputs - outputs
    taps = jnp.arange(TAPS, dtype=jnp.int32)
    hits = (offset[:, :, None] == taps[None, None, :]).astype(jnp.float32)
    return jnp.einsum("oit,t->oi", hits, kernel, precision=HIGH)


def coverage(kernel, shift, count, first, total):
    places = first + jnp.arange(count, dtype=jnp.int32)
    taps = jnp.arange(TAPS, dtype=jnp.int32)
    source = places[:, None] - taps[None, :] + (TAPS - 1) // 2 - shift
    inside = ((source >= 0) & (source < total)).astype(jnp.float32)
    return jnp.sum(inside * kernel[None, :], axis=1)


def along(band, volume):
    return jnp.einsum("oi,iyx->oyx", band, volume, precision=NEAR)


def lateral(volume, matrix_y, matrix_x):
    moved = jnp.einsum("yi,zix->zyx", matrix_y, volume, precision=NEAR)
    return jnp.einsum("zyi,xi->zyx", moved, matrix_x, precision=NEAR)


def lateral_back(volume, matrix_y, matrix_x):
    moved = jnp.einsum("iy,zix->zyx", matrix_y, volume, precision=NEAR)
    return jnp.einsum("zyi,ix->zyx", moved, matrix_x, precision=NEAR)


def swap(value, bit):
    count = lax.axis_size("view")
    return lax.ppermute(value, "view", [(i, i ^ bit) for i in range(count)])


def to_next(value):
    count = lax.axis_size("blk")
    return lax.ppermute(value, "blk", [(i, i + 1) for i in range(count - 1)])


def to_previous(value):
    count = lax.axis_size("blk")
    return lax.ppermute(value, "blk", [(i + 1, i) for i in range(count - 1)])


def pack_kernel(slot_ref, tiles_ref, out_ref):
    def step(i, carry):
        out_ref[slot_ref[i]] = tiles_ref[i]
        return carry

    lax.fori_loop(0, tiles_ref.shape[0], step, 0)


def pack(slot, tiles, slots):
    count, rows, width = tiles.shape
    return pl.pallas_call(
        pack_kernel,
        out_shape=jax.ShapeDtypeStruct((slots, rows, width), jnp.float32),
        in_specs=[
            pl.BlockSpec(memory_space=pltpu.SMEM),
            pl.BlockSpec(memory_space=pltpu.VMEM),
        ],
        out_specs=pl.BlockSpec(memory_space=pltpu.VMEM),
        compiler_params=pltpu.CompilerParams(vmem_limit_bytes=24 << 20),
        cost_estimate=pl.CostEstimate(flops=0, transcendentals=0, bytes_accessed=12 * tiles.size),
    )(slot, tiles)


def assemble_kernel(start_ref, filled_ref, values_ref, out_ref):
    rows, width = values_ref.shape[1:]
    cells = out_ref.shape[0]
    out_ref[...] = jnp.zeros_like(out_ref)

    def step(i, carry):
        @pl.when(filled_ref[i] > 0)
        def _():
            start = start_ref[i]
            base = pl.multiple_of(jnp.minimum(start // 8 * 8, cells - rows - 8), 8)
            tile = jnp.concatenate([values_ref[i], jnp.zeros((8, width), jnp.float32)], axis=0)
            place = pl.ds(base, rows + 8)
            out_ref[place, :] = out_ref[place, :] + pltpu.roll(tile, start - base, 0)

        return carry

    lax.fori_loop(0, values_ref.shape[0], step, 0)


def assemble(start, filled, values, cells):
    width = values.shape[2]
    return pl.pallas_call(
        assemble_kernel,
        out_shape=jax.ShapeDtypeStruct((cells, width), jnp.float32),
        in_specs=[
            pl.BlockSpec(memory_space=pltpu.SMEM),
            pl.BlockSpec(memory_space=pltpu.SMEM),
            pl.BlockSpec(memory_space=pltpu.VMEM),
        ],
        out_specs=pl.BlockSpec(memory_space=pltpu.VMEM),
        compiler_params=pltpu.CompilerParams(vmem_limit_bytes=40 << 20),
        cost_estimate=pl.CostEstimate(
            flops=values.size, transcendentals=0, bytes_accessed=4 * (values.size + cells * width)
        ),
    )(start, filled, values)


def per_device(estimate, tiles, tile_dest, tile_plane, tile_row, psf, view_shift):
    blocks = lax.axis_size("blk")
    block_index = lax.axis_index("blk")
    view_index = lax.axis_index("view")
    low, high = view_index % 2, view_index // 2
    planes, height, width = estimate.shape
    tile_dev = tiles.shape[1]
    tile_rows = tiles.shape[2]
    capacity = max(2, 2 * tile_dev // blocks)
    radius = (TAPS - 1) // 2
    target_all = tile_dest[0, :, 0].reshape(blocks, tile_dev)
    own_target = lax.dynamic_index_in_dim(target_all, block_index, 0, keepdims=False)
    block_ids = jnp.arange(blocks, dtype=jnp.int32)
    onehot = (own_target[:, None] == block_ids[None, :]).astype(jnp.int32)
    earlier = jnp.cumsum(onehot, axis=0) - onehot
    rank = jnp.sum(earlier * onehot, axis=1)
    slot = own_target * capacity + rank
    outgoing = pack(slot, tiles[0], blocks * capacity)
    outgoing = outgoing.reshape(blocks, capacity, tile_rows, width)
    incoming = lax.all_to_all(outgoing, "blk", split_axis=0, concat_axis=0, tiled=True)
    quarter = height // 4
    first = (low * 2 + high) * quarter
    strip = lax.dynamic_slice_in_dim(estimate, first, quarter, 1)
    above = to_next(strip[planes - radius :])
    below = to_previous(strip[:radius])
    mine = jnp.concatenate([above, below], axis=0)
    theirs = swap(mine, 2)
    half = jnp.concatenate([mine, theirs], axis=1)
    other_half = swap(half, 1)
    halo = jnp.concatenate([half, other_half], axis=1)

    kernels = normalize(psf)
    own_kernel = lax.dynamic_index_in_dim(kernels, view_index, 0, keepdims=False)
    own_shift = lax.dynamic_index_in_dim(view_shift, view_index, 0, keepdims=False)
    matrix_y = lateral_matrix(own_kernel[1], own_shift[0], height)
    matrix_x = lateral_matrix(own_kernel[2], own_shift[1], width)
    parts = matrix_y.reshape(height, 2, 2, quarter)
    parts = jnp.where(low == 0, parts, parts[:, ::-1])
    first_pair = jnp.where(high == 0, parts[:, 0], parts[:, 0, ::-1])
    second_pair = jnp.where(high == 0, parts[:, 1], parts[:, 1, ::-1])
    matrix_halo = jnp.stack([first_pair, second_pair], axis=1).reshape(height, height)

    landing = (target_all == block_index).astype(jnp.int32)
    order = jnp.cumsum(landing, axis=1) - landing
    slot_ids = jnp.arange(capacity, dtype=jnp.int32)
    picks = landing[:, :, None] * (order[:, :, None] == slot_ids[None, None, :]).astype(jnp.int32)
    plane_all = tile_plane[0].reshape(blocks, tile_dev)
    row_all = tile_row[0].reshape(blocks, tile_dev)
    filled = jnp.sum(picks, axis=1).reshape(-1)
    plane = jnp.sum(picks * plane_all[:, :, None], axis=1).reshape(-1)
    row = jnp.sum(picks * row_all[:, :, None], axis=1).reshape(-1)
    values = incoming.reshape(blocks * capacity, tile_rows, width)
    total = assemble(plane * height + row, filled, values, planes * height)
    at_plane = (plane[:, None] == jnp.arange(planes, dtype=jnp.int32)) & (filled[:, None] > 0)
    offset = jnp.arange(height, dtype=jnp.int32)[None, :] - row[:, None]
    at_row = (offset >= 0) & (offset < tile_rows)
    count = jnp.einsum("sz,sy->zy", at_plane.astype(jnp.float32), at_row.astype(jnp.float32), precision=HIGH)
    data = total.reshape(planes, height, width) / jnp.maximum(count, 1.0)[:, :, None]

    forward_band = band_matrix(own_kernel[0], planes)
    back_band = band_matrix(own_kernel[0], planes)
    own_image = lateral(estimate, matrix_y, matrix_x)
    own_image = along(forward_band[:, radius : radius + planes], own_image)
    edge_band = jnp.concatenate([forward_band[:, :radius], forward_band[:, radius + planes :]], axis=1)
    image = own_image + along(edge_band, lateral(halo, matrix_halo, matrix_x))
    ratio = data / (image + BACKGROUND)

    covers = []
    for other in range(psf.shape[0]):
        covers.append((
            coverage(kernels[other, 0], 0, planes, block_index * planes, planes * blocks),
            coverage(kernels[other, 1], view_shift[other, 0], height, 0, height),
            coverage(kernels[other, 2], view_shift[other, 1], width, 0, width),
        ))
    chunk = height // CHUNKS
    rows = chunk // 2
    spread = back_band.T
    halves, others = [], []
    for k in range(CHUNKS):
        part = lateral_back(ratio, matrix_y[:, k * chunk : (k + 1) * chunk], matrix_x)
        wide = along(spread, part)
        kept = jnp.where(low == 0, wide[:, :rows], wide[:, rows:])
        given = jnp.where(low == 0, wide[:, rows:], wide[:, :rows])
        pair = kept + swap(given, 1)
        from_next = to_previous(pair[:radius])
        from_previous = to_next(pair[radius + planes :])
        own = pair[radius : radius + planes]
        nothing = jnp.zeros((planes - radius, rows, width), jnp.float32)
        own = own + jnp.concatenate([from_previous, nothing], axis=0)
        own = own + jnp.concatenate([nothing, from_next], axis=0)
        full = own + swap(own, 2)
        start = k * chunk + low * rows
        sensitivity = jnp.zeros((planes, rows, width), jnp.float32)
        for cover_z, cover_y, cover_x in covers:
            piece = lax.dynamic_slice_in_dim(cover_y, start, rows, 0)
            sensitivity = sensitivity + cover_z[:, None, None] * piece[None, :, None] * cover_x[None, None, :]
        current = lax.dynamic_slice_in_dim(estimate, start, rows, 1)
        done = current * full / sensitivity
        halves.append(done)
        others.append(swap(done, 1))
    pieces = []
    for mine, theirs in zip(halves, others):
        pieces.append(jnp.where(low == 0, mine, theirs))
        pieces.append(jnp.where(low == 0, theirs, mine))
    return jnp.concatenate(pieces, axis=1)


def solution(mesh):
    in_specs = (
        P("blk", None, None),
        P("view", "blk", None, None),
        P("view", None, None),
        P("view", None),
        P("view", None),
        P(),
        P(),
    )
    out_specs = P("blk", None, None)
    return jax.shard_map(
        per_device, mesh=mesh, in_specs=in_specs, out_specs=out_specs, check_vma=False
    )
```

```python
import jax
import jax.numpy as jnp
from jax import lax
from jax.experimental import pallas as pl
from jax.experimental.pallas import tpu as pltpu
from jax.sharding import PartitionSpec as P

TAPS = 31


HIGH = lax.Precision.HIGHEST
NEAR = lax.Precision.HIGH
BACKGROUND = 0.05
CHUNKS = 4
STRIPS = 2


def normalize(psf):
    return psf / jnp.sum(psf, axis=-1, keepdims=True)


def lateral_matrix(kernel, shift, count):
    outputs = jnp.arange(count, dtype=jnp.int32)[:, None]
    inputs = jnp.arange(count, dtype=jnp.int32)[None, :]
    offset = inputs - outputs + (TAPS - 1) // 2 - shift
    taps = jnp.arange(TAPS, dtype=jnp.int32)
    hits = (offset[:, :, None] == taps[None, None, :]).astype(jnp.float32)
    return jnp.einsum("oit,t->oi", hits, kernel, precision=HIGH)


def band_matrix(kernel, rows):
    outputs = jnp.arange(rows, dtype=jnp.int32)[:, None]
    inputs = jnp.arange(rows + TAPS - 1, dtype=jnp.int32)[None, :]
    offset = inputs - outputs
    taps = jnp.arange(TAPS, dtype=jnp.int32)
    hits = (offset[:, :, None] == taps[None, None, :]).astype(jnp.float32)
    return jnp.einsum("oit,t->oi", hits, kernel, precision=HIGH)


def coverage(kernel, shift, count, first, total):
    places = first + jnp.arange(count, dtype=jnp.int32)
    taps = jnp.arange(TAPS, dtype=jnp.int32)
    source = places[:, None] - taps[None, :] + (TAPS - 1) // 2 - shift
    inside = ((source >= 0) & (source < total)).astype(jnp.float32)
    return jnp.sum(inside * kernel[None, :], axis=1)


def along(band, volume):
    return jnp.einsum("oi,iyx->oyx", band, volume, precision=NEAR)


def lateral(volume, matrix_y, matrix_x):
    moved = jnp.einsum("yi,zix->zyx", matrix_y, volume, precision=NEAR)
    return jnp.einsum("zyi,xi->zyx", moved, matrix_x, precision=NEAR)


def swap(value, bit):
    count = lax.axis_size("view")
    return lax.ppermute(value, "view", [(i, i ^ bit) for i in range(count)])


def to_next(value):
    count = lax.axis_size("blk")
    return lax.ppermute(value, "blk", [(i, i + 1) for i in range(count - 1)])


def to_previous(value):
    count = lax.axis_size("blk")
    return lax.ppermute(value, "blk", [(i + 1, i) for i in range(count - 1)])


def pack_kernel(slot_ref, tiles_ref, out_ref):
    def step(i, carry):
        out_ref[slot_ref[i]] = tiles_ref[i]
        return carry

    lax.fori_loop(0, tiles_ref.shape[0], step, 0)


def pack(slot, tiles, slots):
    _, rows, width = tiles.shape
    return pl.pallas_call(
        pack_kernel,
        out_shape=jax.ShapeDtypeStruct((slots, rows, width), jnp.float32),
        in_specs=[
            pl.BlockSpec(memory_space=pltpu.SMEM),
            pl.BlockSpec(memory_space=pltpu.VMEM),
        ],
        out_specs=pl.BlockSpec(memory_space=pltpu.VMEM),
        compiler_params=pltpu.CompilerParams(vmem_limit_bytes=24 << 20),
        cost_estimate=pl.CostEstimate(flops=0, transcendentals=0, bytes_accessed=12 * tiles.size),
    )(slot, tiles)


def assemble_kernel(start_ref, filled_ref, values_ref, out_ref):
    rows, width = values_ref.shape[1:]
    cells = out_ref.shape[0]
    out_ref[...] = jnp.zeros_like(out_ref)

    def step(i, carry):
        @pl.when(filled_ref[i] > 0)
        def _():
            start = start_ref[i]
            base = pl.multiple_of(jnp.minimum(start // 8 * 8, cells - rows - 8), 8)
            tile = jnp.concatenate([values_ref[i], jnp.zeros((8, width), jnp.float32)], axis=0)
            place = pl.ds(base, rows + 8)
            out_ref[place, :] = out_ref[place, :] + pltpu.roll(tile, start - base, 0)

        return carry

    lax.fori_loop(0, values_ref.shape[0], step, 0)


def assemble(start, filled, values, cells):
    width = values.shape[2]
    return pl.pallas_call(
        assemble_kernel,
        out_shape=jax.ShapeDtypeStruct((cells, width), jnp.float32),
        in_specs=[
            pl.BlockSpec(memory_space=pltpu.SMEM),
            pl.BlockSpec(memory_space=pltpu.SMEM),
            pl.BlockSpec(memory_space=pltpu.VMEM),
        ],
        out_specs=pl.BlockSpec(memory_space=pltpu.VMEM),
        compiler_params=pltpu.CompilerParams(vmem_limit_bytes=40 << 20),
        cost_estimate=pl.CostEstimate(
            flops=values.size, transcendentals=0, bytes_accessed=4 * (values.size + cells * width)
        ),
    )(start, filled, values)


def per_device(estimate, tiles, tile_dest, tile_plane, tile_row, psf, view_shift):
    blocks = lax.axis_size("blk")
    block_index = lax.axis_index("blk")
    view_index = lax.axis_index("view")
    low, high = view_index % 2, view_index // 2
    planes, height, width = estimate.shape
    tile_dev = tiles.shape[1]
    tile_rows = tiles.shape[2]
    capacity = max(2, 2 * tile_dev // blocks)
    radius = (TAPS - 1) // 2
    target_all = tile_dest[0, :, 0].reshape(blocks, tile_dev)
    own_target = lax.dynamic_index_in_dim(target_all, block_index, 0, keepdims=False)
    block_ids = jnp.arange(blocks, dtype=jnp.int32)
    onehot = (own_target[:, None] == block_ids[None, :]).astype(jnp.int32)
    earlier = jnp.cumsum(onehot, axis=0) - onehot
    rank = jnp.sum(earlier * onehot, axis=1)
    slot = own_target * capacity + rank
    outgoing = pack(slot, tiles[0], blocks * capacity)
    outgoing = outgoing.reshape(blocks, capacity, tile_rows, width)
    incoming = lax.all_to_all(outgoing, "blk", split_axis=0, concat_axis=0, tiled=True)
    piece = height // (4 * STRIPS)
    arrivals = []
    for s in range(STRIPS):
        first = ((low * STRIPS + s) * 2 + high) * piece
        strip = lax.dynamic_slice_in_dim(estimate, first, piece, 1)
        tail, front = strip[planes - radius :], strip[:radius]
        if s:
            tail, front, above, below = lax.optimization_barrier((tail, front, above, below))
            arrivals.append((above, below))
        above, below = to_next(tail), to_previous(front)
    arrivals.append((above, below))
    kernels = normalize(psf)
    own_kernel = lax.dynamic_index_in_dim(kernels, view_index, 0, keepdims=False)
    own_shift = lax.dynamic_index_in_dim(view_shift, view_index, 0, keepdims=False)
    matrix_y = lateral_matrix(own_kernel[1], own_shift[0], height)
    matrix_x = lateral_matrix(own_kernel[2], own_shift[1], width)
    parts = matrix_y.reshape(height, 2, STRIPS, 2, piece)
    parts = jnp.where(low == 0, parts, parts[:, ::-1])
    parts = jnp.where(high == 0, parts, parts[:, :, :, ::-1])
    matrix_halo = parts.reshape(height, height)
    forward_band = band_matrix(own_kernel[0], planes)
    own_image = lateral(estimate, matrix_y, matrix_x)
    own_image = along(forward_band[:, radius : radius + planes], own_image)

    above, below, own_image, matrix_halo = lax.optimization_barrier(
        arrivals[-1] + (own_image, matrix_halo)
    )
    arrivals[-1] = (above, below)
    halves, other_halves = [], []
    for above, below in arrivals:
        mine = jnp.concatenate([above, below], axis=0)
        half = jnp.concatenate([mine, swap(mine, 2)], axis=1)
        halves.append(half)
        other_halves.append(swap(half, 1))
    halo = jnp.concatenate(halves + other_halves, axis=1)

    landing = (target_all == block_index).astype(jnp.int32)
    order = jnp.cumsum(landing, axis=1) - landing
    slot_ids = jnp.arange(capacity, dtype=jnp.int32)
    picks = landing[:, :, None] * (order[:, :, None] == slot_ids[None, None, :]).astype(jnp.int32)
    plane_all = tile_plane[0].reshape(blocks, tile_dev)
    row_all = tile_row[0].reshape(blocks, tile_dev)
    filled = jnp.sum(picks, axis=1).reshape(-1)
    plane = jnp.sum(picks * plane_all[:, :, None], axis=1).reshape(-1)
    row = jnp.sum(picks * row_all[:, :, None], axis=1).reshape(-1)
    values = incoming.reshape(blocks * capacity, tile_rows, width)
    total = assemble(plane * height + row, filled, values, planes * height)
    at_plane = (plane[:, None] == jnp.arange(planes, dtype=jnp.int32)) & (filled[:, None] > 0)
    offset = jnp.arange(height, dtype=jnp.int32)[None, :] - row[:, None]
    at_row = (offset >= 0) & (offset < tile_rows)
    count = jnp.einsum("sz,sy->zy", at_plane.astype(jnp.float32), at_row.astype(jnp.float32), precision=HIGH)
    data = total.reshape(planes, height, width) / jnp.maximum(count, 1.0)[:, :, None]

    back_band = forward_band
    edge_band = jnp.concatenate([forward_band[:, :radius], forward_band[:, radius + planes :]], axis=1)
    image = own_image + along(edge_band, lateral(halo, matrix_halo, matrix_x))
    ratio = data / (image + BACKGROUND)

    covers = []
    for other in range(psf.shape[0]):
        covers.append((
            coverage(kernels[other, 0], 0, planes, block_index * planes, planes * blocks),
            coverage(kernels[other, 1], view_shift[other, 0], height, 0, height),
            coverage(kernels[other, 2], view_shift[other, 1], width, 0, width),
        ))
    chunk = height // CHUNKS
    rows = chunk // 2
    spread = back_band.T
    halves, others = [], []
    moved = jnp.einsum("iy,zix->zyx", matrix_y, ratio, precision=NEAR)
    pairs = []
    for k in range(CHUNKS):
        part = moved[:, k * chunk : (k + 1) * chunk]
        wide = along(spread, jnp.einsum("zyi,ix->zyx", part, matrix_x, precision=NEAR))
        kept = jnp.where(low == 0, wide[:, :rows], wide[:, rows:])
        given = jnp.where(low == 0, wide[:, rows:], wide[:, :rows])
        pairs.append(kept + swap(given, 1))
    nothing = jnp.zeros((planes - radius, rows, width), jnp.float32)
    sums = []
    for k in range(CHUNKS):
        pair = pairs[k]
        if k:
            pair, from_next, from_previous = lax.optimization_barrier((pair, from_next, from_previous))
            own = own + jnp.concatenate([from_previous, nothing], axis=0)
            sums.append(own + jnp.concatenate([nothing, from_next], axis=0))
        if k:
            pair, sums[k - 1] = lax.optimization_barrier((pair, sums[k - 1]))
        from_next = to_previous(pair[:radius])
        from_previous = to_next(pair[radius + planes :])
        own = pair[radius : radius + planes]
    own = own + jnp.concatenate([from_previous, nothing], axis=0)
    sums.append(own + jnp.concatenate([nothing, from_next], axis=0))
    for k in range(CHUNKS):
        own = sums[k]
        received = swap(own, 2)
        full = own + received
        start = k * chunk + low * rows
        sensitivity = jnp.zeros((planes, rows, width), jnp.float32)
        for cover_z, cover_y, cover_x in covers:
            piece = lax.dynamic_slice_in_dim(cover_y, start, rows, 0)
            sensitivity = sensitivity + cover_z[:, None, None] * piece[None, :, None] * cover_x[None, None, :]
        current = lax.dynamic_slice_in_dim(estimate, start, rows, 1)
        done = current * full / sensitivity
        halves.append(done)
        others.append(swap(done, 1))
    pieces = []
    for mine, theirs in zip(halves, others):
        pieces.append(jnp.where(low == 0, mine, theirs))
        pieces.append(jnp.where(low == 0, theirs, mine))
    return jnp.concatenate(pieces, axis=1)


def solution(mesh):
    in_specs = (
        P("blk", None, None),
        P("view", "blk", None, None),
        P("view", None, None),
        P("view", None),
        P("view", None),
        P(),
        P(),
    )
    out_specs = P("blk", None, None)

    return jax.shard_map(
        per_device, mesh=mesh, in_specs=in_specs, out_specs=out_specs, check_vma=False
    )
```

```python
import jax
import jax.numpy as jnp
from jax import lax
from jax.experimental.layout import Layout, with_layout_constraint
from jax.experimental import pallas as pl
from jax.experimental.pallas import tpu as pltpu
from jax.sharding import PartitionSpec as P

TAPS = 31


HIGH = lax.Precision.HIGHEST
NEAR = lax.Precision.HIGH
BACKGROUND = 0.05
CHUNKS = 4
STRIPS = 2
WINDOW = 2


def normalize(psf):
    return psf / jnp.sum(psf, axis=-1, keepdims=True)


def lateral_matrix(kernel, shift, count):
    outputs = jnp.arange(count, dtype=jnp.int32)[:, None]
    inputs = jnp.arange(count, dtype=jnp.int32)[None, :]
    offset = inputs - outputs + (TAPS - 1) // 2 - shift
    taps = jnp.arange(TAPS, dtype=jnp.int32)
    hits = (offset[:, :, None] == taps[None, None, :]).astype(jnp.float32)
    return jnp.einsum("oit,t->oi", hits, kernel, precision=HIGH)


def band_matrix(kernel, rows):
    outputs = jnp.arange(rows, dtype=jnp.int32)[:, None]
    inputs = jnp.arange(rows + TAPS - 1, dtype=jnp.int32)[None, :]
    offset = inputs - outputs
    taps = jnp.arange(TAPS, dtype=jnp.int32)
    hits = (offset[:, :, None] == taps[None, None, :]).astype(jnp.float32)
    return jnp.einsum("oit,t->oi", hits, kernel, precision=HIGH)


def coverage(kernel, shift, count, first, total):
    places = first + jnp.arange(count, dtype=jnp.int32)
    taps = jnp.arange(TAPS, dtype=jnp.int32)
    source = places[:, None] - taps[None, :] + (TAPS - 1) // 2 - shift
    inside = ((source >= 0) & (source < total)).astype(jnp.float32)
    return jnp.sum(inside * kernel[None, :], axis=1)


def along(band, volume):
    return jnp.einsum("oi,iyx->oyx", band, volume, precision=NEAR)


def lateral(volume, matrix_y, matrix_x):
    moved = jnp.einsum("yi,zix->zyx", matrix_y, volume, precision=NEAR)
    return jnp.einsum("zyi,xi->zyx", moved, matrix_x, precision=NEAR)


def row_major(value):
    return with_layout_constraint(value, Layout(major_to_minor=(0, 1, 2)))


def swap(value, bit):
    count = lax.axis_size("view")
    return lax.ppermute(value, "view", [(i, i ^ bit) for i in range(count)])


def to_next(value):
    count = lax.axis_size("blk")
    return lax.ppermute(value, "blk", [(i, i + 1) for i in range(count - 1)])


def to_previous(value):
    count = lax.axis_size("blk")
    return lax.ppermute(value, "blk", [(i + 1, i) for i in range(count - 1)])


def pack_kernel(slot_ref, tiles_ref, out_ref):
    def step(i, carry):
        out_ref[slot_ref[i]] = tiles_ref[i]
        return carry

    lax.fori_loop(0, tiles_ref.shape[0], step, 0)


def pack(slot, tiles, slots):
    _, rows, width = tiles.shape
    return pl.pallas_call(
        pack_kernel,
        out_shape=jax.ShapeDtypeStruct((slots, rows, width), jnp.float32),
        in_specs=[
            pl.BlockSpec(memory_space=pltpu.SMEM),
            pl.BlockSpec(memory_space=pltpu.VMEM),
        ],
        out_specs=pl.BlockSpec(memory_space=pltpu.VMEM),
        compiler_params=pltpu.CompilerParams(vmem_limit_bytes=24 << 20),
        cost_estimate=pl.CostEstimate(flops=0, transcendentals=0, bytes_accessed=12 * tiles.size),
    )(slot, tiles)


def assemble_kernel(start_ref, filled_ref, values_ref, out_ref):
    rows, width = values_ref.shape[1:]
    cells = out_ref.shape[0]
    out_ref[...] = jnp.zeros_like(out_ref)

    def step(i, carry):
        @pl.when(filled_ref[i] > 0)
        def _():
            start = start_ref[i]
            base = pl.multiple_of(jnp.minimum(start // 8 * 8, cells - rows - 8), 8)
            tile = jnp.concatenate([values_ref[i], jnp.zeros((8, width), jnp.float32)], axis=0)
            place = pl.ds(base, rows + 8)
            out_ref[place, :] = out_ref[place, :] + pltpu.roll(tile, start - base, 0)

        return carry

    lax.fori_loop(0, values_ref.shape[0], step, 0)


def assemble(start, filled, values, cells):
    width = values.shape[2]
    return pl.pallas_call(
        assemble_kernel,
        out_shape=jax.ShapeDtypeStruct((cells, width), jnp.float32),
        in_specs=[
            pl.BlockSpec(memory_space=pltpu.SMEM),
            pl.BlockSpec(memory_space=pltpu.SMEM),
            pl.BlockSpec(memory_space=pltpu.VMEM),
        ],
        out_specs=pl.BlockSpec(memory_space=pltpu.VMEM),
        compiler_params=pltpu.CompilerParams(vmem_limit_bytes=40 << 20),
        cost_estimate=pl.CostEstimate(
            flops=values.size, transcendentals=0, bytes_accessed=4 * (values.size + cells * width)
        ),
    )(start, filled, values)


def per_device(estimate, tiles, tile_dest, tile_plane, tile_row, psf, view_shift):
    blocks = lax.axis_size("blk")
    block_index = lax.axis_index("blk")
    view_index = lax.axis_index("view")
    low, high = view_index % 2, view_index // 2
    planes, height, width = estimate.shape
    tile_dev = tiles.shape[1]
    tile_rows = tiles.shape[2]
    capacity = max(2, 2 * tile_dev // blocks)
    radius = (TAPS - 1) // 2
    target_all = tile_dest[0, :, 0].reshape(blocks, tile_dev)
    own_target = lax.dynamic_index_in_dim(target_all, block_index, 0, keepdims=False)
    block_ids = jnp.arange(blocks, dtype=jnp.int32)
    onehot = (own_target[:, None] == block_ids[None, :]).astype(jnp.int32)
    earlier = jnp.cumsum(onehot, axis=0) - onehot
    rank = jnp.sum(earlier * onehot, axis=1)
    slot = own_target * capacity + rank
    outgoing = pack(slot, tiles[0], blocks * capacity)
    outgoing = outgoing.reshape(blocks, capacity, tile_rows, width)
    incoming = lax.all_to_all(outgoing, "blk", split_axis=0, concat_axis=0, tiled=True)
    piece = height // (4 * STRIPS)
    arrivals = []
    for s in range(STRIPS):
        first = ((low * STRIPS + s) * 2 + high) * piece
        strip = lax.dynamic_slice_in_dim(estimate, first, piece, 1)
        tail, front = strip[planes - radius :], strip[:radius]
        if s:
            tail, front, above, below = lax.optimization_barrier((tail, front, above, below))
            arrivals.append((above, below))
        above, below = to_next(tail), to_previous(front)
    arrivals.append((above, below))
    kernels = normalize(psf)
    own_kernel = lax.dynamic_index_in_dim(kernels, view_index, 0, keepdims=False)
    own_shift = lax.dynamic_index_in_dim(view_shift, view_index, 0, keepdims=False)
    matrix_y = lateral_matrix(own_kernel[1], own_shift[0], height)
    matrix_x = lateral_matrix(own_kernel[2], own_shift[1], width)
    parts = matrix_y.reshape(height, 2, STRIPS, 2, piece)
    parts = jnp.where(low == 0, parts, parts[:, ::-1])
    parts = jnp.where(high == 0, parts, parts[:, :, :, ::-1])
    matrix_halo = parts.reshape(height, height)
    forward_band = band_matrix(own_kernel[0], planes)
    own_image = lateral(estimate, matrix_y, matrix_x)
    own_image = along(forward_band[:, radius : radius + planes], own_image)

    above, below, own_image, matrix_halo = lax.optimization_barrier(
        arrivals[-1] + (own_image, matrix_halo)
    )
    arrivals[-1] = (above, below)
    halves, other_halves = [], []
    for above, below in arrivals:
        mine = jnp.concatenate([above, below], axis=0)
        half = jnp.concatenate([mine, swap(mine, 2)], axis=1)
        halves.append(half)
        other_halves.append(swap(half, 1))
    halo = row_major(jnp.concatenate(halves + other_halves, axis=1))

    landing = (target_all == block_index).astype(jnp.int32)
    order = jnp.cumsum(landing, axis=1) - landing
    slot_ids = jnp.arange(capacity, dtype=jnp.int32)
    picks = landing[:, :, None] * (order[:, :, None] == slot_ids[None, None, :]).astype(jnp.int32)
    plane_all = tile_plane[0].reshape(blocks, tile_dev)
    row_all = tile_row[0].reshape(blocks, tile_dev)
    filled = jnp.sum(picks, axis=1).reshape(-1)
    plane = jnp.sum(picks * plane_all[:, :, None], axis=1).reshape(-1)
    row = jnp.sum(picks * row_all[:, :, None], axis=1).reshape(-1)
    values = incoming.reshape(blocks * capacity, tile_rows, width)
    total = assemble(plane * height + row, filled, values, planes * height)
    at_plane = (plane[:, None] == jnp.arange(planes, dtype=jnp.int32)) & (filled[:, None] > 0)
    offset = jnp.arange(height, dtype=jnp.int32)[None, :] - row[:, None]
    at_row = (offset >= 0) & (offset < tile_rows)
    count = jnp.einsum("sz,sy->zy", at_plane.astype(jnp.float32), at_row.astype(jnp.float32), precision=HIGH)
    data = total.reshape(planes, height, width) / jnp.maximum(count, 1.0)[:, :, None]

    back_band = forward_band
    edge_band = jnp.concatenate([forward_band[:, :radius], forward_band[:, radius + planes :]], axis=1)
    image = own_image + along(edge_band, lateral(halo, matrix_halo, matrix_x))
    ratio = data / (image + BACKGROUND)

    covers = []
    for other in range(psf.shape[0]):
        covers.append((
            coverage(kernels[other, 0], 0, planes, block_index * planes, planes * blocks),
            coverage(kernels[other, 1], view_shift[other, 0], height, 0, height),
            coverage(kernels[other, 2], view_shift[other, 1], width, 0, width),
        ))
    chunk = height // CHUNKS
    rows = chunk // 2
    spread = back_band.T
    halves, others = [], []
    moved = jnp.einsum("iy,zix->zyx", matrix_y, ratio, precision=NEAR)
    pairs = []
    for k in range(CHUNKS):
        part = moved[:, k * chunk : (k + 1) * chunk]
        wide = along(spread, jnp.einsum("zyi,ix->zyx", part, matrix_x, precision=NEAR))
        kept = jnp.where(low == 0, wide[:, :rows], wide[:, rows:])
        given = jnp.where(low == 0, wide[:, rows:], wide[:, :rows])
        pairs.append(row_major(kept + swap(given, 1)))
    nothing = jnp.zeros((planes - radius, rows, width), jnp.float32)
    flights, sums = [], []

    def landed(k):
        own, from_next, from_previous = flights[k]
        own = own + jnp.concatenate([from_previous, nothing], axis=0)
        return own + jnp.concatenate([nothing, from_next], axis=0)

    for k in range(CHUNKS):
        pair = pairs[k]
        if k >= WINDOW:
            pair, total_sum = lax.optimization_barrier((pair, landed(k - WINDOW)))
            sums.append(total_sum)
        from_next = to_previous(pair[:radius])
        from_previous = to_next(pair[radius + planes :])
        flights.append((pair[radius : radius + planes], from_next, from_previous))
    for k in range(CHUNKS - WINDOW, CHUNKS):
        sums.append(landed(k))
    for k in range(CHUNKS):
        own = sums[k]
        received = swap(own, 2)
        full = own + received
        start = k * chunk + low * rows
        sensitivity = jnp.zeros((planes, rows, width), jnp.float32)
        for cover_z, cover_y, cover_x in covers:
            piece = lax.dynamic_slice_in_dim(cover_y, start, rows, 0)
            sensitivity = sensitivity + cover_z[:, None, None] * piece[None, :, None] * cover_x[None, None, :]
        current = lax.dynamic_slice_in_dim(estimate, start, rows, 1)
        done = current * full / sensitivity
        halves.append(done)
        others.append(swap(done, 1))
    pieces = []
    for mine, theirs in zip(halves, others):
        pieces.append(jnp.where(low == 0, mine, theirs))
        pieces.append(jnp.where(low == 0, theirs, mine))
    return jnp.concatenate(pieces, axis=1)


def solution(mesh):
    in_specs = (
        P("blk", None, None),
        P("view", "blk", None, None),
        P("view", None, None),
        P("view", None),
        P("view", None),
        P(),
        P(),
    )
    out_specs = P("blk", None, None)

    return jax.shard_map(
        per_device, mesh=mesh, in_specs=in_specs, out_specs=out_specs, check_vma=False
    )
```
